512 devices in a mesh: dp: 8 (over z_hi, x), expert: 64 (over z_lo, y, core).
Axes of the slice: x: 4, y: 8, z: 8 (z_hi: 2, z_lo: 4; z = z_hi * 4 + z_lo), core: 2. Of those that a mesh axis runs over, the one named last changes fastest.
Arguments:
- features: bfloat16 [8192, 3584], P('expert', 'dp'), may hold values from -6 to 6
- upstream: bfloat16 [8192, 3584], P('expert', 'dp'), may hold values from -6 to 6
- expert_ids: int32 [8192, 8], P('expert'), may hold values from 0 to 63, all different within a row
- gate_probs: float32 [8192, 8], P('expert'), may hold values from 0.02 to 0.5
- capacity: int32 [64], replicated, may hold values from 1 to 16, as said below
- up_weight: bfloat16 [64, 3584, 1024], P('expert', 'dp'), may hold values from -5 to 5
- down_weight: bfloat16 [64, 1024, 3584], P('expert', None, 'dp'), may hold values from -5 to 5
- round_noise: bfloat16 [64, 3584, 1024], P('expert', 'dp'), may hold values from 0 to 1
Outputs:
- mixed: bfloat16 [8192, 3584], P('expert', 'dp')
- grad_tokens: bfloat16 [8192, 3584], P('expert', 'dp')
- new_up: bfloat16 [64, 3584, 1024], P('expert', 'dp')
- new_down: bfloat16 [64, 1024, 3584], P('expert', None, 'dp')
The draws below stay inside these ranges and needn't reach their ends.
Inputs may be any that keep to these rules, and one draw needn't show every extreme that they name: Experts 64/2 .. 63 have capacity 12 + 1 to 16; experts 0 .. 31 have capacity 12 - 4 or less; some expert has exactly 16, and some exactly 8.
All inputs are finite; a program needn't handle non-finite values.
Results may differ from the reference program's by a relative error of at most 0.025.
Values may be sent and summed in bfloat16 or wider, within the bound.
A program may use at most 64 MiB of HBM per device.

```python
import math
import jax
import jax.numpy as jnp
from jax import lax

D = 3584
FFN = 1024
TOPK = 8
TOK_DEV = 128
EXPERTS = 64
TOKENS = 8192
SLOT_BLOCK = 4
CAP = 12
N_DP = 8
N_EXPERT = 64


def draw_capacity(key, part):
    pair_count = EXPERTS // 2
    subkeys = jax.random.split(key, 4)
    forced_hot = jax.random.randint(subkeys[0], (), 0, pair_count)
    forced_help = jax.random.randint(subkeys[1], (), 0, pair_count)
    pair_index = jnp.arange(pair_count)
    hot_caps = jax.random.randint(subkeys[2], (pair_count,), CAP + 1, CAP + SLOT_BLOCK + 1)
    hot_caps = jnp.where(pair_index == forced_hot, CAP + SLOT_BLOCK, hot_caps)
    help_caps = jax.random.randint(subkeys[3], (pair_count,), 1, CAP - SLOT_BLOCK + 1)
    help_caps = jnp.where(pair_index == forced_help, CAP - SLOT_BLOCK, help_caps)
    return jnp.concatenate([help_caps, hot_caps]).astype(jnp.int32)


def block_scale(key, dims, shards, smallest, largest):
    gain = 1.0
    for axis_at, blocks in shards:
        draws = jax.random.uniform(jax.random.fold_in(jax.random.fold_in(key, 6), axis_at), (blocks,), jnp.float32, smallest / len(shards), largest / len(shards))
        gain = gain * jnp.repeat(jnp.exp(draws), dims[axis_at] // blocks).reshape((-1,) + (1,) * (len(dims) - 1 - axis_at))
    return gain


def different_ones(rng, rows, number_of, top, lift):
    order = jax.random.permutation(jax.random.fold_in(rng, 1), number_of)
    boost = order
    for power in range(3):
        boost = boost * boost // number_of
    boost = boost * lift // number_of
    lots = jax.random.randint(jax.random.fold_in(rng, 2), (rows, number_of), 0, 4096) + boost
    sure = jax.random.permutation(jax.random.fold_in(rng, 3), rows)[jnp.arange(number_of) % rows]
    lots = jnp.where(jnp.arange(rows)[:, None] == sure[None, :], 1 << 14, lots)
    priority = lots * number_of + jnp.arange(number_of)
    return lax.top_k(priority.astype(jnp.int32), top)[1].astype(jnp.int32)


def scatter_about(own_key, dims, scale, limit, cuts=(), kind=jnp.bfloat16):
    values = jax.random.normal(own_key, dims, jnp.float32) * scale
    if len(cuts) > 0:
        values = block_scale(own_key, dims, cuts, -0.22, 0.18) * values
    return jnp.clip(values, min=-limit, max=limit).astype(kind)


def setup_inputs(seed: int = 0) -> dict:
    arg_keys = jax.random.split(jax.random.key(seed), 9)
    return {
        "features": scatter_about(arg_keys[0], (TOKENS, D), 1.0, 6.0, ((0, 64), (1, 8))),
        "upstream": scatter_about(arg_keys[1], (TOKENS, D), 1.0, 6.0, ((0, 64), (1, 8))),
        "expert_ids": different_ones(arg_keys[2], TOKENS, EXPERTS, TOPK, 2048),
        "gate_probs": jnp.clip(jnp.exp(math.log(0.5) - 3.218876 * jax.random.uniform(arg_keys[3], (TOKENS, TOPK), jnp.float32) ** block_scale(arg_keys[3], (TOKENS, TOPK), ((0, 64),), -0.2, 0.2)), 0.02, 0.5),
        "capacity": draw_capacity(jax.random.fold_in(arg_keys[8], 71), 0),
        "up_weight": scatter_about(arg_keys[5], (EXPERTS, D, FFN), 1.0, 5.0, ((0, 64), (1, 8))),
        "down_weight": scatter_about(arg_keys[6], (EXPERTS, FFN, D), 1.0, 5.0, ((0, 64), (2, 8))),
        "round_noise": jnp.clip(1.0 * jax.random.uniform(arg_keys[7], (EXPERTS, D, FFN), jnp.float32) ** block_scale(arg_keys[7], (EXPERTS, D, FFN), ((0, 64), (1, 8)), -0.2, 0.2), 0.0, 1.0).astype(jnp.bfloat16),
    }


step_size = 4.0
noise_width = 0.25


def silu_slope(pre_act):
    sigmoid = jax.nn.sigmoid(pre_act)
    return sigmoid * (1.0 + pre_act * (1.0 - sigmoid))


def stochastic(weights, grads, noise):
    target = weights.astype(jnp.float32) - step_size * grads
    spacing = noise_width * jnp.abs(target)
    return (target + (noise.astype(jnp.float32) - 0.5) * spacing).astype(jnp.bfloat16)


def rounded_sum(terms):
    narrow = lax.optimization_barrier(terms.astype(jnp.bfloat16))
    return jnp.sum(narrow.astype(jnp.float32), axis=1)


def reference(features, upstream, expert_ids, gate_probs, capacity, up_weight, down_weight, round_noise):
    block_count = N_EXPERT
    most_rows = CAP + SLOT_BLOCK
    assign_count = TOK_DEV * TOPK
    group_feat = D // N_DP
    up_scale = D ** -0.5
    down_scale = FFN ** -0.5
    ids_block = expert_ids.reshape(block_count, assign_count)
    probs_block = gate_probs.reshape(block_count, assign_count)
    feat_block = features.reshape(block_count, TOK_DEV, D)
    cot_block = upstream.reshape(block_count, TOK_DEV, D)
    columns = jnp.arange(EXPERTS, dtype=jnp.int32)
    onehot = (ids_block[:, :, None] == columns[None, None, :]).astype(jnp.int32)
    ranking = jnp.sum((jnp.cumsum(onehot, axis=1) - onehot) * onehot, axis=2)
    limits = jnp.sum(onehot * capacity[None, None, :], axis=2)
    kept = ranking < limits
    order = jnp.arange(assign_count, dtype=jnp.int32)
    row_range = jnp.arange(most_rows, dtype=jnp.int32)
    block_index = jnp.arange(block_count, dtype=jnp.int32)[:, None]

    def per_expert(carry, inputs):
        mixed_acc, grad_acc = carry
        expert, w_in, w_out, noise_in = inputs
        match_rows = (ids_block == expert) & kept
        hits = match_rows[:, :, None] & (ranking[:, :, None] == row_range[None, None, :])
        valid = jnp.any(hits, axis=1)
        chosen = jnp.sum(jnp.where(hits, order[None, :, None], 0), axis=1).astype(jnp.int32)
        token_pos = (chosen // TOPK).astype(jnp.int32)
        prob_sel = jnp.where(valid, jnp.take_along_axis(probs_block, chosen, axis=1), 0.0)
        feat_rows = jnp.take_along_axis(feat_block, token_pos[:, :, None], axis=1).astype(jnp.float32)
        feat_rows = jnp.where(valid[:, :, None], feat_rows, 0.0)
        cot_rows = jnp.take_along_axis(cot_block, token_pos[:, :, None], axis=1).astype(jnp.float32)
        grad_rows = (prob_sel[:, :, None] * cot_rows).astype(jnp.bfloat16).astype(jnp.float32)
        rows_x = feat_rows.reshape(-1, N_DP, group_feat)
        rows_g = grad_rows.reshape(-1, N_DP, group_feat)
        w_in32 = w_in.astype(jnp.float32).reshape(N_DP, group_feat, FFN)
        w_out32 = w_out.astype(jnp.float32).reshape(FFN, N_DP, group_feat)
        pre = rounded_sum(jnp.einsum("rid,idf->rif", rows_x, w_in32) * up_scale)
        act = jax.nn.silu(pre).astype(jnp.bfloat16)
        act32 = act.astype(jnp.float32)
        outs = (jnp.einsum("rf,fid->rid", act32, w_out32) * down_scale).astype(jnp.bfloat16)
        dact = rounded_sum(jnp.einsum("rid,fid->rif", rows_g, w_out32) * down_scale)
        dpre = (dact * silu_slope(pre)).astype(jnp.bfloat16)
        dpre32 = dpre.astype(jnp.float32)
        dxs = (jnp.einsum("rf,idf->rid", dpre32, w_in32) * up_scale).astype(jnp.bfloat16)
        grad_in = jnp.einsum("rid,rf->idf", rows_x, dpre32).reshape(D, FFN) * up_scale
        grad_out = jnp.einsum("rf,rid->fid", act32, rows_g).reshape(FFN, D) * down_scale
        new_in = stochastic(w_in, grad_in, noise_in)
        new_out = stochastic(w_out, grad_out, noise_in.T)
        contrib = prob_sel[:, :, None] * outs.reshape(block_count, most_rows, D).astype(jnp.float32)
        back_rows = jnp.where(valid[:, :, None], dxs.reshape(block_count, most_rows, D).astype(jnp.float32), 0.0)
        mixed_acc = mixed_acc.at[block_index, token_pos].add(contrib)
        grad_acc = grad_acc.at[block_index, token_pos].add(back_rows)
        return (mixed_acc, grad_acc), (new_in, new_out)

    start = jnp.zeros((block_count, TOK_DEV, D), jnp.float32)
    (mixed_acc, grad_acc), (new_up, new_down) = lax.scan(
        per_expert, (start, start), (columns, up_weight, down_weight, round_noise))
    mixed = mixed_acc.reshape(TOKENS, D).astype(jnp.bfloat16)
    grad_tokens = grad_acc.reshape(TOKENS, D).astype(jnp.bfloat16)
    return (mixed, grad_tokens, new_up, new_down)
```

```python
import functools

import jax
import jax.numpy as jnp
from jax import lax
from jax.experimental import pallas as pl
from jax.experimental.pallas import tpu as pltpu
from jax.sharding import PartitionSpec as P

D = 3584
FFN = 1024
LOC = 448
WIDE = 2 * LOC
EXPERTS = 64
HALF = EXPERTS // 2
TOK = 128
COLD = 8
HOT = 16
COLD_ROWS = HALF * COLD
SLOTS = HALF * (COLD + HOT)
MAX_ROWS = EXPERTS * HOT
CR = 256
HR = CR // 2
NC = MAX_ROWS // CR
PLANE = 16
UP_SCALE = D ** -0.5
DOWN_SCALE = FFN ** -0.5
STEP = 4.0
NOISE = 0.25
F32 = jnp.float32
BF16 = jnp.bfloat16


def contract(a, b, da, db):
    return lax.dot_general(a, b, (((da,), (db,)), ((), ())), preferred_element_type=F32)


def stochastic(weights, grads, noise):
    target = weights.astype(F32) - STEP * grads
    return (target + (noise.astype(F32) - 0.5) * (NOISE * jnp.abs(target))).astype(BF16)


def kernel(
    both, ids_ref, probs_ref, cap_ref, up, down, noise,
    mixed, grad_tok, new_up, new_down,
    pick, phi, plo, packed, xg, ups, dnp, part, r1, r2, r3, ad, back, got, gup, gdn, noise_t,
    disp_send, disp_recv, step_send, step_recv, ret_send, ret_recv,
):
    dp = lax.axis_index("dp")
    me = lax.axis_index("expert")
    plane = me // PLANE
    inplane = lax.rem(me, PLANE)
    hot = me >= HALF
    x = lax.rem(dp, 4)
    z_hi = dp // 4
    bit_a = lax.rem((x + 1) // 2, 2)
    bit_b = x // 2
    peer_a = z_hi * 4 + (x + 1 - 2 * lax.rem(x, 2))
    peer_b = z_hi * 4 + (3 - x)
    peer_z = (1 - z_hi) * 4 + x

    barrier = pltpu.get_barrier_semaphore()

    @pl.loop(1, EXPERTS)
    def _(j):
        pl.semaphore_signal(barrier, inc=1, device_id=(dp, lax.rem(me + j, EXPERTS)),
                            device_id_type=pl.DeviceIdType.MESH)

    for peer in (peer_a, peer_b, peer_z):
        pl.semaphore_signal(barrier, inc=1, device_id=(peer, me),
                            device_id_type=pl.DeviceIdType.MESH)

    lanes_e = lax.broadcasted_iota(jnp.int32, (TOK, EXPERTS), 1)
    chosen = jnp.zeros((TOK, EXPERTS), F32)
    prob = jnp.zeros((TOK, EXPERTS), F32)
    for k in range(8):
        hit = ids_ref[:, k:k + 1] == lanes_e
        chosen = chosen + jnp.where(hit, 1.0, 0.0)
        prob = prob + jnp.where(hit, probs_ref[:, k:k + 1], 0.0)
    earlier = jnp.where(
        lax.broadcasted_iota(jnp.int32, (TOK, TOK), 0)
        > lax.broadcasted_iota(jnp.int32, (TOK, TOK), 1), 1.0, 0.0).astype(BF16)
    rank = jnp.dot(earlier, chosen.astype(BF16), preferred_element_type=F32)
    kept = jnp.where((chosen > 0.5) & (rank < cap_ref[...].astype(F32)), rank, -1.0).astype(BF16)
    prob_hi = prob.astype(BF16)
    prob_lo = (prob - prob_hi.astype(F32)).astype(BF16)
    for i in range(SLOTS // TOK):
        rows = pl.ds(i * TOK, TOK)
        r_e = lax.broadcasted_iota(jnp.int32, (TOK, EXPERTS), 0) + i * TOK
        r_t = lax.broadcasted_iota(jnp.int32, (TOK, TOK), 0) + i * TOK
        if i * TOK < COLD_ROWS:
            expert_of, slot_of = r_e // COLD, lax.rem(r_t, COLD)
        else:
            expert_of, slot_of = r_e // HOT + COLD_ROWS // HOT, lax.rem(r_t, HOT)
        spread = jnp.where(expert_of == lanes_e, 1.0, 0.0).astype(BF16)
        match = contract(spread, kept, 1, 1) == slot_of.astype(F32)
        sel = jnp.where(match, 1.0, 0.0).astype(BF16)
        w_hi = jnp.where(match, contract(spread, prob_hi, 1, 1), 0.0).astype(BF16)
        w_lo = jnp.where(match, contract(spread, prob_lo, 1, 1), 0.0).astype(BF16)
        pick[rows, :] = sel
        phi[rows, :] = w_hi
        plo[rows, :] = w_lo
        g = (jnp.dot(w_hi, both[:, 0:512], preferred_element_type=F32)
             + jnp.dot(w_lo, both[:, 0:512], preferred_element_type=F32))
        f = jnp.dot(sel, both[:, 384:WIDE], preferred_element_type=F32)
        lane = lax.broadcasted_iota(jnp.int32, (TOK, 128), 1)
        packed[rows, 0:384] = g[:, 0:384].astype(BF16)
        packed[rows, 384:512] = jnp.where(lane < 64, g[:, 384:512], f[:, 0:128]).astype(BF16)
        packed[rows, 512:WIDE] = f[:, 128:512].astype(BF16)

    pl.semaphore_wait(barrier, EXPERTS - 1 + 3)

    def send_plane(to_plane, count, first):
        @pl.loop(0, PLANE)
        def _(j):
            dest = to_plane * PLANE + lax.rem(inplane + j, PLANE)
            src = packed.at[pl.ds(pl.multiple_of(first + dest * count, 8), count)]
            dst = xg.at[pl.ds(pl.multiple_of(me * count, 8), count)]
            sem = disp_recv.at[(me * count) // CR]

            @pl.when(dest != me)
            def _():
                pltpu.make_async_remote_copy(
                    src_ref=src, dst_ref=dst, send_sem=disp_send, recv_sem=sem,
                    device_id=(dp, dest), device_id_type=pl.DeviceIdType.MESH).start()

            @pl.when(dest == me)
            def _():
                pltpu.make_async_copy(src, dst, sem).start()

    first_hot = jnp.where(hot, plane, 3 - plane)
    first_cold = jnp.where(hot, 3 - plane, plane)
    send_plane(first_hot, HOT, COLD_ROWS - HALF * HOT)
    send_plane(5 - first_hot, HOT, COLD_ROWS - HALF * HOT)
    send_plane(first_cold, COLD, 0)
    send_plane(1 - first_cold, COLD, 0)

    ups[0:64, :] = jnp.zeros((64, FFN), BF16)
    ups[64:512, :] = up[...]
    dnp[:, 384:512] = jnp.zeros((FFN, 128), BF16)
    dnp[:, 0:LOC] = down[...]

    def exchange(stage, q, h):
        first, second = (peer_a, peer_b) if h == 0 else (peer_b, peer_a)
        b1, b2 = (bit_a, bit_b) if h == 0 else (bit_b, bit_a)
        n1, n2, n3 = HR // 2, HR // 4, HR // 8
        if stage == 0:
            src, dst, peer = part.at[q, pl.ds(pl.multiple_of(n1 * (1 - b1), n1), n1)], r1.at[q], first
        elif stage == 1:
            src, dst, peer = r1.at[q, pl.ds(pl.multiple_of(n2 * (1 - b2), n2), n2)], r2.at[q], second
        elif stage == 2:
            src, dst, peer = r2.at[q, pl.ds(pl.multiple_of(n3 * (1 - z_hi), n3), n3)], r3.at[q], peer_z
        elif stage == 3:
            src = ad.at[q, pl.ds(pl.multiple_of(n1 * b1 + n2 * b2 + n3 * z_hi, n3), n3)]
            dst, peer = src, peer_z
        elif stage == 4:
            src = ad.at[q, pl.ds(pl.multiple_of(n1 * b1 + n2 * b2, n2), n2)]
            dst, peer = src, second
        else:
            src = ad.at[q, pl.ds(pl.multiple_of(n1 * b1, n1), n1)]
            dst, peer = src, first
        return pltpu.make_async_remote_copy(
            src_ref=src, dst_ref=dst, send_sem=step_send.at[stage, q],
            recv_sem=step_recv.at[stage, q], device_id=(peer, me),
            device_id_type=pl.DeviceIdType.MESH)

    chunks = jnp.where(hot, NC, NC // 2)

    def chunk_at(i):
        order = jnp.where(i == 0, plane, jnp.where(i == 1, 5 - plane, jnp.where(i == 2, 3 - plane, plane - 2)))
        return jnp.where(hot, order, i)

    def products_in(ci):
        whole = xg.at[pl.ds(pl.multiple_of(ci * CR, CR), CR)]
        pltpu.make_async_copy(whole, whole, disp_recv.at[ci]).wait()
        for h in range(2):
            q = ci * 2 + h
            rows = pl.ds(pl.multiple_of(ci * CR + h * HR, HR), HR)
            part[q, :, 0:FFN] = (contract(xg[rows, 384:WIDE], ups[...], 1, 0) * UP_SCALE).astype(BF16)
            part[q, :, FFN:2 * FFN] = (contract(xg[rows, 0:512], dnp[...], 1, 1) * DOWN_SCALE).astype(BF16)
            exchange(0, q, h).start()

    def add_first(ci):
        for h in range(2):
            q = ci * 2 + h
            n1 = HR // 2
            b1 = bit_a if h == 0 else bit_b
            exchange(0, q, h).wait_recv()
            keep = pl.ds(pl.multiple_of(n1 * b1, n1), n1)
            r1[q] = (r1[q].astype(F32) + part[q, keep, :].astype(F32)).astype(BF16)
            exchange(1, q, h).start()

    def add_second(ci):
        for h in range(2):
            q = ci * 2 + h
            n2 = HR // 4
            b2 = bit_b if h == 0 else bit_a
            exchange(1, q, h).wait_recv()
            keep = pl.ds(pl.multiple_of(n2 * b2, n2), n2)
            r2[q] = (r2[q].astype(F32) + r1[q, keep, :].astype(F32)).astype(BF16)
            exchange(2, q, h).start()

    def activate(ci):
        for h in range(2):
            q = ci * 2 + h
            n1, n2, n3 = HR // 2, HR // 4, HR // 8
            b1, b2 = (bit_a, bit_b) if h == 0 else (bit_b, bit_a)
            exchange(2, q, h).wait_recv()
            keep = pl.ds(pl.multiple_of(n3 * z_hi, n3), n3)
            total = r3[q].astype(F32) + r2[q, keep, :].astype(F32)
            pre, dact = total[:, 0:FFN], total[:, FFN:2 * FFN]
            s = 1.0 / (1.0 + jnp.exp(-pre))
            rows = pl.ds(pl.multiple_of(n1 * b1 + n2 * b2 + n3 * z_hi, n3), n3)
            ad[q, rows, 0:FFN] = (pre * s).astype(BF16)
            ad[q, rows, FFN:2 * FFN] = (dact * (s * (1.0 + pre * (1.0 - s)))).astype(BF16)
            exchange(3, q, h).start()

    def pass_on(stage, ci):
        for h in range(2):
            q = ci * 2 + h
            exchange(stage - 1, q, h).wait_recv()
            exchange(stage, q, h).start()

    def send_back(base, count, first):
        @pl.loop(0, HR // count)
        def _(j):
            dest = base // count + j
            src = back.at[pl.ds(pl.multiple_of(base + j * count, 8), count)]
            dst = got.at[pl.ds(pl.multiple_of(first + me * count, 8), count)]

            @pl.when(dest != me)
            def _():
                pltpu.make_async_remote_copy(
                    src_ref=src, dst_ref=dst, send_sem=ret_send, recv_sem=ret_recv,
                    device_id=(dp, dest), device_id_type=pl.DeviceIdType.MESH).start()

            @pl.when(dest == me)
            def _():
                pltpu.make_async_copy(src, dst, ret_recv).start()

    def products_out(ci):
        for h in range(2):
            q = ci * 2 + h
            base = ci * CR + h * HR
            rows = pl.ds(pl.multiple_of(base, HR), HR)
            exchange(5, q, h).wait_recv()
            y = contract(ad[q, :, 0:FFN], dnp[...], 1, 0) * DOWN_SCALE
            d = contract(ad[q, :, FFN:2 * FFN], ups[...], 1, 1) * UP_SCALE
            back[rows, 0:384] = y[:, 0:384].astype(BF16)
            back[rows, 384:512] = (y[:, 384:512] + d[:, 0:128]).astype(BF16)
            back[rows, 512:WIDE] = d[:, 128:512].astype(BF16)

            @pl.when(hot)
            def _():
                send_back(base, HOT, COLD_ROWS - HALF * HOT)

            @pl.when(jnp.logical_not(hot))
            def _():
                send_back(base, COLD, 0)

        for h in range(2):
            q = ci * 2 + h
            rows = pl.ds(pl.multiple_of(ci * CR + h * HR, HR), HR)

            @pl.loop(0, FFN // 256)
            def _(t):
                cols = pl.ds(pl.multiple_of(t * 256, 256), 256)
                cols_d = pl.ds(pl.multiple_of(FFN + t * 256, 256), 256)
                gup[:, cols] += contract(xg[rows, 384:WIDE], ad[q, :, cols_d], 0, 0)
                gdn[cols, :] += contract(ad[q, :, cols], xg[rows, 0:512], 0, 0)

    gup[...] = jnp.zeros_like(gup)
    gdn[...] = jnp.zeros_like(gdn)
    eye = jnp.where(
        lax.broadcasted_iota(jnp.int32, (128, 128), 0)
        == lax.broadcasted_iota(jnp.int32, (128, 128), 1), 1.0, 0.0).astype(BF16)

    @pl.loop(0, FFN // 128)
    def _(t):
        cols = pl.ds(pl.multiple_of(t * 128, 128), 128)
        noise_t[cols, :] = contract(eye, noise[:, cols], 1, 1).astype(BF16)

    stages = [
        products_in, add_first, add_second, activate,
        functools.partial(pass_on, 4), functools.partial(pass_on, 5), products_out,
    ]

    @pl.loop(0, chunks + len(stages) - 1)
    def _(t):
        for s in reversed(range(len(stages))):
            i = t - s

            @pl.when((i >= 0) & (i < chunks))
            def _(s=s, i=i):
                stages[s](chunk_at(i))

    @pl.loop(0, 7)
    def _(t):
        rows = pl.ds(pl.multiple_of(t * 64, 64), 64)
        rows_g = pl.ds(pl.multiple_of(t * 64 + 64, 64), 64)
        new_up[rows, :] = stochastic(up[rows, :], UP_SCALE * gup[rows_g, :], noise[rows, :])

    @pl.loop(0, 8)
    def _(t):
        rows = pl.ds(pl.multiple_of(t * 128, 128), 128)
        new_down[rows, :] = stochastic(down[rows, :], DOWN_SCALE * gdn[rows, 0:LOC], noise_t[rows, :])

    pltpu.make_async_copy(got, got, ret_recv).wait()
    m = contract(phi[...], got[:, 0:512], 0, 0) + contract(plo[...], got[:, 0:512], 0, 0)
    mixed[...] = m[:, 0:LOC].astype(BF16)
    grad_tok[...] = contract(pick[...], got[:, 384:WIDE], 0, 0).astype(BF16)

    @pl.loop(0, chunks)
    def _(c):
        for h in range(2):
            for stage in range(6):
                exchange(stage, c * 2 + h, h).wait_send()

    def drain(sent, returned):
        a = packed.at[pl.ds(0, sent)]
        pltpu.make_async_copy(a, a, disp_send).wait()
        b = back.at[pl.ds(0, returned)]
        pltpu.make_async_copy(b, b, ret_send).wait()

    @pl.when(hot)
    def _():
        drain(SLOTS - HOT, EXPERTS * HOT - HOT)

    @pl.when(jnp.logical_not(hot))
    def _():
        drain(SLOTS - COLD, EXPERTS * COLD - COLD)


def shards(
    features, upstream, expert_ids, gate_probs, capacity, up_weight, down_weight, round_noise
):
    both = jnp.concatenate([upstream, features], axis=1)
    vmem = pl.BlockSpec(memory_space=pltpu.VMEM)
    shape = jax.ShapeDtypeStruct
    mixed, grad_tok, new_up, new_down = pl.pallas_call(
        kernel,
        out_shape=(
            shape((TOK, LOC), BF16), shape((TOK, 512), BF16),
            shape((LOC, FFN), BF16), shape((FFN, LOC), BF16),
        ),
        in_specs=[vmem] * 7,
        out_specs=(vmem,) * 4,
        scratch_shapes=[
            pltpu.VMEM((SLOTS, TOK), BF16),
            pltpu.VMEM((SLOTS, TOK), BF16),
            pltpu.VMEM((SLOTS, TOK), BF16),
            pltpu.VMEM((SLOTS, WIDE), BF16),
            pltpu.VMEM((MAX_ROWS, WIDE), BF16),
            pltpu.VMEM((512, FFN), BF16),
            pltpu.VMEM((FFN, 512), BF16),
            pltpu.VMEM((2 * NC, HR, 2 * FFN), BF16),
            pltpu.VMEM((2 * NC, HR // 2, 2 * FFN), BF16),
            pltpu.VMEM((2 * NC, HR // 4, 2 * FFN), BF16),
            pltpu.VMEM((2 * NC, HR // 8, 2 * FFN), BF16),
            pltpu.VMEM((2 * NC, HR, 2 * FFN), BF16),
            pltpu.VMEM((MAX_ROWS, WIDE), BF16),
            pltpu.VMEM((SLOTS, WIDE), BF16),
            pltpu.VMEM((512, FFN), F32),
            pltpu.VMEM((FFN, 512), F32),
            pltpu.VMEM((FFN, LOC), BF16),
            pltpu.SemaphoreType.DMA,
            pltpu.SemaphoreType.DMA((NC,)),
            pltpu.SemaphoreType.DMA((6, 2 * NC)),
            pltpu.SemaphoreType.DMA((6, 2 * NC)),
            pltpu.SemaphoreType.DMA,
            pltpu.SemaphoreType.DMA,
        ],
        compiler_params=pltpu.CompilerParams(
            collective_id=0, has_side_effects=True, vmem_limit_bytes=56 * 1024 * 1024),
    )(both, expert_ids, gate_probs, capacity.reshape(1, EXPERTS),
      up_weight[0], down_weight[0], round_noise[0])
    return mixed, grad_tok[:, 64:], new_up[None], new_down[None]


def solution(mesh):
    in_specs = (
        P("expert", "dp"),
        P("expert", "dp"),
        P("expert", None),
        P("expert", None),
        P(),
        P("expert", "dp", None),
        P("expert", None, "dp"),
        P("expert", "dp", None),
    )
    out_specs = (
        P("expert", "dp"),
        P("expert", "dp"),
        P("expert", "dp", None),
        P("expert", None, "dp"),
    )
    return jax.shard_map(shards, mesh=mesh, in_specs=in_specs, out_specs=out_specs, check_vma=False)
```

```python
import jax
import jax.numpy as jnp
from jax import lax
from jax.experimental import pallas as pl
from jax.experimental.pallas import tpu as pltpu
from jax.sharding import PartitionSpec as P

D = 3584
FFN = 1024
LOC = 448
WIDE = 2 * LOC
EXPERTS = 64
HALF = EXPERTS // 2
TOK = 128
COLD = 8
HOT = 16
MAX_ROWS = EXPERTS * HOT
CR = 128
QR = CR // 4
NC = MAX_ROWS // CR
PAD = 512
PLANE = 16
PLANES = EXPERTS // PLANE
UP_SCALE = D ** -0.5
DOWN_SCALE = FFN ** -0.5
STEP = 4.0
NOISE = 0.25
F32 = jnp.float32
BF16 = jnp.bfloat16


def contract(a, b, da, db):
    return lax.dot_general(a, b, (((da,), (db,)), ((), ())), preferred_element_type=F32)


def stochastic(weights, grads, noise):
    target = weights.astype(F32) - STEP * grads
    return (target + (noise.astype(F32) - 0.5) * (NOISE * jnp.abs(target))).astype(BF16)


def kernel(
    feat, cot, ids_ref, probs_ref, cap_ref, up_hbm, down_hbm, noise_hbm,
    mixed, grad_tok, new_up, new_down,
    fpad, cpad, ids_all, probs_all, pick, phi, plo, packed, xg, ups, dnp, noise, part, r1, r2, r3,
    ad, back, got, half_out, sums,
    load_sem, share_send, share_recv, disp_send, disp_recv, step_send, step_recv, ret_send, ret_recv,
    sum_send, sum_recv,
):
    dp = lax.axis_index("dp")
    me = lax.axis_index("expert")
    plane = me // PLANE
    inplane = lax.rem(me, PLANE)
    hot = me >= HALF
    x = lax.rem(dp, 4)
    z_hi = dp // 4
    bit_a = lax.rem((x + 1) // 2, 2)
    bit_b = x // 2
    peer_a = z_hi * 4 + (x + 1 - 2 * lax.rem(x, 2))
    peer_b = z_hi * 4 + (3 - x)
    peer_z = (1 - z_hi) * 4 + x

    barrier = pltpu.get_barrier_semaphore()

    def other_plane(d):
        return lax.rem(plane + d, PLANES)

    @pl.loop(1, PLANE)
    def _(j):
        pl.semaphore_signal(barrier, inc=1,
                            device_id=(dp, plane * PLANE + lax.rem(inplane + j, PLANE)),
                            device_id_type=pl.DeviceIdType.MESH)

    @pl.loop(1, PLANES)
    def _(d):
        pl.semaphore_signal(barrier, inc=1, device_id=(dp, other_plane(d) * PLANE + inplane),
                            device_id_type=pl.DeviceIdType.MESH)

    for peer in (peer_a, peer_b, peer_z):
        pl.semaphore_signal(barrier, inc=1, device_id=(peer, me),
                            device_id_type=pl.DeviceIdType.MESH)

    loads = [
        pltpu.make_async_copy(up_hbm, ups.at[pl.ds(64, LOC)], load_sem.at[0]),
        pltpu.make_async_copy(down_hbm, dnp.at[pl.ds(0, LOC)], load_sem.at[1]),
        pltpu.make_async_copy(noise_hbm, noise, load_sem.at[2]),
    ]
    for load in loads:
        load.start()

    for p in range(PLANES):
        fpad[p, 0:64, :] = jnp.zeros((64, TOK), BF16)
        cpad[p, LOC:PAD, :] = jnp.zeros((64, TOK), BF16)
    fpad[plane, 64:PAD, :] = feat[...]
    cpad[plane, 0:LOC, :] = cot[...]
    ids_all[plane] = ids_ref[...]
    probs_all[plane] = probs_ref[...]

    def share(d):
        to = other_plane(d)
        pairs = ((ids_ref, ids_all.at[plane]), (probs_ref, probs_all.at[plane]),
                 (cot, cpad.at[plane, pl.ds(0, LOC)]), (feat, fpad.at[plane, pl.ds(64, LOC)]))
        return [pltpu.make_async_remote_copy(
            src_ref=src, dst_ref=dst, send_sem=share_send.at[n, d], recv_sem=share_recv.at[n, d],
            device_id=(dp, to * PLANE + inplane), device_id_type=pl.DeviceIdType.MESH)
            for n, (src, dst) in enumerate(pairs)]

    def source(k):
        return jnp.where(k == 0, plane, jnp.where(
            k == 1, plane + 1 - 2 * lax.rem(plane, 2),
            jnp.where(k == 2, lax.rem(plane + 2, PLANES), 3 - plane)))

    pl.semaphore_wait(barrier, PLANE - 1 + PLANES - 1 + 3)
    for k in range(1, PLANES):
        for copy in share(lax.rem(source(k) - plane + PLANES, PLANES)):
            copy.start()

    row_e = lax.broadcasted_iota(jnp.int32, (EXPERTS, TOK), 0)
    earlier = jnp.where(
        lax.broadcasted_iota(jnp.int32, (TOK, TOK), 0)
        < lax.broadcasted_iota(jnp.int32, (TOK, TOK), 1), 1.0, 0.0).astype(BF16)
    diagonal = (lax.broadcasted_iota(jnp.int32, (EXPERTS, EXPERTS), 0)
                == lax.broadcasted_iota(jnp.int32, (EXPERTS, EXPERTS), 1))
    limit = jnp.sum(jnp.where(diagonal, cap_ref[...].astype(F32), 0.0), axis=1, keepdims=True)

    def pack(p, count):
        chosen = jnp.zeros((EXPERTS, TOK), F32)
        prob = jnp.zeros((EXPERTS, TOK), F32)
        for k in range(8):
            hit = ids_all[p, k:k + 1, :] == row_e
            chosen = chosen + jnp.where(hit, 1.0, 0.0)
            prob = prob + jnp.where(hit, probs_all[p, k:k + 1, :], 0.0)
        rank = jnp.dot(chosen.astype(BF16), earlier, preferred_element_type=F32)
        kept = jnp.where((chosen > 0.5) & (rank < limit), rank, -1.0).astype(BF16)
        prob_hi = prob.astype(BF16)
        prob_lo = (prob - prob_hi.astype(F32)).astype(BF16)
        for i in range(PLANE * count // TOK):
            rows = pl.ds(i * TOK, TOK)
            r_e = lax.broadcasted_iota(jnp.int32, (TOK, EXPERTS), 0) + i * TOK
            lane_e = lax.broadcasted_iota(jnp.int32, (TOK, EXPERTS), 1)
            slot_of = lax.rem(lax.broadcasted_iota(jnp.int32, (TOK, TOK), 0), count)
            spread = jnp.where(r_e // count + plane * PLANE == lane_e, 1.0, 0.0).astype(BF16)
            match = contract(spread, kept, 1, 0) == slot_of.astype(F32)
            sel = jnp.where(match, 1.0, 0.0).astype(BF16)
            w_hi = jnp.where(match, contract(spread, prob_hi, 1, 0), 0.0).astype(BF16)
            w_lo = jnp.where(match, contract(spread, prob_lo, 1, 0), 0.0).astype(BF16)
            pick[p, rows, :] = sel
            phi[p, rows, :] = w_hi
            plo[p, rows, :] = w_lo
            g = contract(w_hi, cpad[p], 1, 1) + contract(w_lo, cpad[p], 1, 1)
            f = contract(sel, fpad[p], 1, 1)
            packed[p, rows, 0:384] = g[:, 0:384].astype(BF16)
            packed[p, rows, 384:512] = (g[:, 384:512] + f[:, 0:128]).astype(BF16)
            packed[p, rows, 512:WIDE] = f[:, 128:512].astype(BF16)

        block = p * PLANE + inplane

        @pl.loop(0, PLANE)
        def _(j):
            place = lax.rem(inplane + j, PLANE)
            src = packed.at[p, pl.ds(pl.multiple_of(place * count, 8), count)]
            dst = xg.at[pl.ds(pl.multiple_of(block * count, 8), count)]
            sem = disp_recv.at[(block * count) // CR]

            @pl.when(place != inplane)
            def _():
                pltpu.make_async_remote_copy(
                    src_ref=src, dst_ref=dst, send_sem=disp_send, recv_sem=sem,
                    device_id=(dp, plane * PLANE + place),
                    device_id_type=pl.DeviceIdType.MESH).start()

            @pl.when(place == inplane)
            def _():
                pltpu.make_async_copy(src, dst, sem).start()

    def pack_any(p):
        @pl.when(hot)
        def _():
            pack(p, HOT)

        @pl.when(jnp.logical_not(hot))
        def _():
            pack(p, COLD)

    pack_any(plane)

    def pack_next(i):
        @pl.when(i < PLANES - 1)
        def _():
            p = source(i + 1)
            d = lax.rem(plane - p + PLANES, PLANES)
            for copy in share(d):
                copy.wait_recv()
            pack_any(p)

    ups[0:64, :] = jnp.zeros((64, FFN), BF16)
    dnp[LOC:PAD, :] = jnp.zeros((64, FFN), BF16)
    for load in loads:
        load.wait()

    def remote(src, dst, stage, c, w, peer):
        return pltpu.make_async_remote_copy(
            src_ref=src, dst_ref=dst, send_sem=step_send.at[stage, c, w],
            recv_sem=step_recv.at[stage, c, w], device_id=(peer, me),
            device_id_type=pl.DeviceIdType.MESH)

    def copies(stage, c):
        if stage == 0:
            return [remote(part.at[c, 0, 1 - bit_a], r1.at[c, 0], 0, c, 0, peer_a),
                    remote(part.at[c, 1, :, 1 - bit_b], r1.at[c, 1], 0, c, 1, peer_b)]
        if stage == 1:
            return [remote(r1.at[c, 0, 1 - bit_b], r2.at[c, 0], 1, c, 0, peer_b),
                    remote(r1.at[c, 1, 1 - bit_a], r2.at[c, 1], 1, c, 1, peer_a)]
        if stage == 2:
            return [remote(r2.at[c], r3.at[c], 2, c, 0, peer_z)]
        if stage == 3:
            q0, q1 = ad.at[0, c, bit_a, bit_b], ad.at[1, c, bit_a, bit_b]
            return [remote(q0, q0, 3, c, 0, peer_b), remote(q1, q1, 3, c, 1, peer_a)]
        h0, h1 = ad.at[0, c, bit_a], ad.at[1, c, :, bit_b]
        return [remote(h0, h0, 4, c, 0, peer_a), remote(h1, h1, 4, c, 1, peer_b)]

    def start(stage, c):
        for copy in copies(stage, c):
            copy.start()

    def arrived(stage, c):
        for copy in copies(stage, c):
            copy.wait_recv()

    def add(u, v):
        return (u.astype(F32) + v.astype(F32)).astype(BF16)

    chunks = jnp.where(hot, NC, NC // 2)

    def chunk_at(i):
        return jnp.where(hot, source(i // 2) * 2 + lax.rem(i, 2), source(i))

    def products_in(i):
        c = chunk_at(i)
        rows = pl.ds(pl.multiple_of(c * CR, CR), CR)
        pltpu.make_async_copy(xg.at[rows], xg.at[rows], disp_recv.at[c]).wait()
        shape = (2, 2, QR, FFN)
        pre = contract(xg[rows, 384:WIDE], ups[...], 1, 0) * UP_SCALE
        part[c, 0] = pre.astype(BF16).reshape(shape)
        dact = contract(xg[rows, 0:PAD], dnp[...], 1, 0) * DOWN_SCALE
        part[c, 1] = dact.astype(BF16).reshape(shape)
        start(0, c)

    def add_first(i):
        c = chunk_at(i)
        arrived(0, c)
        r1[c, 0] = add(r1[c, 0], part[c, 0, bit_a])
        for a in range(2):
            r1[c, 1, a] = add(r1[c, 1, a], part[c, 1, a, bit_b])
        start(1, c)

    def add_second(i):
        c = chunk_at(i)
        arrived(1, c)
        r2[c, 0] = add(r2[c, 0], r1[c, 0, bit_b])
        r2[c, 1] = add(r2[c, 1], r1[c, 1, bit_a])
        start(2, c)

    def activate(i):
        c = chunk_at(i)
        arrived(2, c)
        pre = r3[c, 0].astype(F32) + r2[c, 0].astype(F32)
        dact = r3[c, 1].astype(F32) + r2[c, 1].astype(F32)
        s = 1.0 / (1.0 + jnp.exp(-pre))
        ad[0, c, bit_a, bit_b] = (pre * s).astype(BF16)
        ad[1, c, bit_a, bit_b] = (dact * (s * (1.0 + pre * (1.0 - s)))).astype(BF16)
        start(3, c)

    def pass_half(i):
        c = chunk_at(i)
        arrived(3, c)
        start(4, c)

    def send_back(c, count):
        per = CR // count

        @pl.loop(0, per)
        def _(j):
            block = c * per + j
            p, place = block // PLANE, lax.rem(block, PLANE)
            src = back.at[pl.ds(pl.multiple_of(block * count, 8), count)]
            dst = got.at[p, pl.ds(pl.multiple_of(inplane * count, 8), count)]

            @pl.when(place != inplane)
            def _():
                pltpu.make_async_remote_copy(
                    src_ref=src, dst_ref=dst, send_sem=ret_send, recv_sem=ret_recv.at[p],
                    device_id=(dp, plane * PLANE + place),
                    device_id_type=pl.DeviceIdType.MESH).start()

            @pl.when(place == inplane)
            def _():
                pltpu.make_async_copy(src, dst, ret_recv.at[p]).start()

    def products_out(i):
        c = chunk_at(i)
        arrived(4, c)
        base = c * CR
        rows = pl.ds(pl.multiple_of(base, CR), CR)
        y = contract(ad[0, c].reshape(CR, FFN), dnp[...], 1, 1) * DOWN_SCALE
        d = contract(ad[1, c].reshape(CR, FFN), ups[...], 1, 1) * UP_SCALE
        back[rows, 0:384] = y[:, 0:384].astype(BF16)
        back[rows, 384:512] = (y[:, 384:512] + d[:, 0:128]).astype(BF16)
        back[rows, 512:WIDE] = d[:, 128:512].astype(BF16)

        @pl.when(hot)
        def _():
            send_back(c, HOT)

        @pl.when(jnp.logical_not(hot))
        def _():
            send_back(c, COLD)

    def total_copy(d):
        to = other_plane(d)
        return pltpu.make_async_remote_copy(
            src_ref=half_out.at[to], dst_ref=sums.at[plane], send_sem=sum_send.at[d],
            recv_sem=sum_recv.at[d], device_id=(dp, to * PLANE + inplane),
            device_id_type=pl.DeviceIdType.MESH)

    def combine(p, count):
        n = PLANE * count
        rows = got.at[p, pl.ds(0, n)]
        pltpu.make_async_copy(rows, rows, ret_recv.at[p]).wait()
        out = got[p, 0:n, 0:PAD]
        m = contract(out, phi[p, 0:n, :], 0, 0) + contract(out, plo[p, 0:n, :], 0, 0)
        half_out[p, 0] = m[0:LOC, :].astype(BF16)
        g = contract(got[p, 0:n, 384:WIDE], pick[p, 0:n, :], 0, 0)
        half_out[p, 1] = g[64:PAD, :].astype(BF16)

        @pl.when(p != plane)
        def _():
            total_copy(lax.rem(p - plane + PLANES, PLANES)).start()

    def combine_next(i):
        @pl.when(hot & (lax.rem(i, 2) == 1))
        def _():
            combine(source(i // 2), HOT)

        @pl.when(jnp.logical_not(hot))
        def _():
            combine(source(i), COLD)

    schedule = [
        (add_first, 1), (activate, 2), (products_in, 0), (add_second, 1), (products_out, 3),
        (pass_half, 2), (pack_next, 0), (combine_next, 5),
    ]
    lag_max = max(lag for _, lag in schedule)

    @pl.loop(0, chunks + lag_max)
    def _(t):
        for stage, lag in schedule:
            i = t - lag

            @pl.when((i >= 0) & (i < chunks))
            def _(stage=stage, i=i):
                stage(i)

    def update(count):
        n = count // CR
        act = ad[0, 0:n].reshape(count, FFN)
        dpre = ad[1, 0:n].reshape(count, FFN)
        for i in range(4):
            lo, hi = i * 128, i * 128 + 128
            grad = contract(xg[0:count, 384 + lo:384 + hi], dpre, 0, 0)
            skip = 64 if i == 0 else 0
            new_up[lo + skip - 64:hi - 64, :] = stochastic(
                ups[lo + skip:hi, :], UP_SCALE * grad[skip:, :], noise[lo + skip - 64:hi - 64, :])
            grad = contract(xg[0:count, lo:hi], act, 0, 0)
            hi = min(hi, LOC)
            new_down[lo:hi, :] = stochastic(
                dnp[lo:hi, :], DOWN_SCALE * grad[0:hi - lo, :], noise[lo:hi, :])

    @pl.when(hot)
    def _():
        update(MAX_ROWS)

    @pl.when(jnp.logical_not(hot))
    def _():
        update(EXPERTS * COLD)

    m = half_out[plane, 0].astype(F32)
    g = half_out[plane, 1].astype(F32)
    for d in range(1, PLANES):
        total_copy(d).wait_recv()
        p = lax.rem(plane - d + PLANES, PLANES)
        m = m + sums[p, 0].astype(F32)
        g = g + sums[p, 1].astype(F32)
    mixed[...] = m.astype(BF16)
    grad_tok[...] = g.astype(BF16)

    @pl.loop(0, chunks)
    def _(c):
        for stage in range(5):
            for copy in copies(stage, c):
                copy.wait_send()

    for d in range(1, PLANES):
        total_copy(d).wait_send()
        for copy in share(d):
            copy.wait_send()

    def drain(count):
        sent = back.at[pl.ds(0, PLANES * (PLANE - 1) * count)]
        pltpu.make_async_copy(sent, sent, disp_send).wait()
        pltpu.make_async_copy(sent, sent, ret_send).wait()

    @pl.when(hot)
    def _():
        drain(HOT)

    @pl.when(jnp.logical_not(hot))
    def _():
        drain(COLD)


def shards(
    features, upstream, expert_ids, gate_probs, capacity, up_weight, down_weight, round_noise
):
    vmem = pl.BlockSpec(memory_space=pltpu.VMEM)
    hbm = pl.BlockSpec(memory_space=pl.ANY)
    shape = jax.ShapeDtypeStruct
    mixed, grad_tok, new_up, new_down = pl.pallas_call(
        kernel,
        out_shape=(
            shape((LOC, TOK), BF16), shape((LOC, TOK), BF16),
            shape((LOC, FFN), BF16), shape((LOC, FFN), BF16),
        ),
        in_specs=[vmem] * 5 + [hbm] * 3,
        out_specs=(vmem,) * 4,
        scratch_shapes=[
            pltpu.VMEM((PLANES, PAD, TOK), BF16),
            pltpu.VMEM((PLANES, PAD, TOK), BF16),
            pltpu.VMEM((PLANES, 8, TOK), jnp.int32),
            pltpu.VMEM((PLANES, 8, TOK), F32),
            pltpu.VMEM((PLANES, PLANE * HOT, TOK), BF16),
            pltpu.VMEM((PLANES, PLANE * HOT, TOK), BF16),
            pltpu.VMEM((PLANES, PLANE * HOT, TOK), BF16),
            pltpu.VMEM((PLANES, PLANE * HOT, WIDE), BF16),
            pltpu.VMEM((MAX_ROWS, WIDE), BF16),
            pltpu.VMEM((PAD, FFN), BF16),
            pltpu.VMEM((PAD, FFN), BF16),
            pltpu.VMEM((LOC, FFN), BF16),
            pltpu.VMEM((NC, 2, 2, 2, QR, FFN), BF16),
            pltpu.VMEM((NC, 2, 2, QR, FFN), BF16),
            pltpu.VMEM((NC, 2, QR, FFN), BF16),
            pltpu.VMEM((NC, 2, QR, FFN), BF16),
            pltpu.VMEM((2, NC, 2, 2, QR, FFN), BF16),
            pltpu.VMEM((MAX_ROWS, WIDE), BF16),
            pltpu.VMEM((PLANES, PLANE * HOT, WIDE), BF16),
            pltpu.VMEM((PLANES, 2, LOC, TOK), BF16),
            pltpu.VMEM((PLANES, 2, LOC, TOK), BF16),
            pltpu.SemaphoreType.DMA((3,)),
            pltpu.SemaphoreType.DMA((4, PLANES)),
            pltpu.SemaphoreType.DMA((4, PLANES)),
            pltpu.SemaphoreType.DMA,
            pltpu.SemaphoreType.DMA((NC,)),
            pltpu.SemaphoreType.DMA((5, NC, 2)),
            pltpu.SemaphoreType.DMA((5, NC, 2)),
            pltpu.SemaphoreType.DMA,
            pltpu.SemaphoreType.DMA((PLANES,)),
            pltpu.SemaphoreType.DMA((PLANES,)),
            pltpu.SemaphoreType.DMA((PLANES,)),
        ],
        compiler_params=pltpu.CompilerParams(
            collective_id=0, has_side_effects=True, vmem_limit_bytes=56 * 1024 * 1024),
    )(features.T, upstream.T, expert_ids.T, gate_probs.T, capacity.reshape(1, EXPERTS),
      up_weight[0], down_weight[0].T, round_noise[0])
    return mixed.T, grad_tok.T, new_up[None], new_down.T[None]


def solution(mesh):
    in_specs = (
        P("expert", "dp"),
        P("expert", "dp"),
        P("expert", None),
        P("expert", None),
        P(),
        P("expert", "dp", None),
        P("expert", None, "dp"),
        P("expert", "dp", None),
    )
    out_specs = (
        P("expert", "dp"),
        P("expert", "dp"),
        P("expert", "dp", None),
        P("expert", None, "dp"),
    )
    return jax.shard_map(shards, mesh=mesh, in_specs=in_specs, out_specs=out_specs, check_vma=False)
```

```python
import jax
import jax.numpy as jnp
from jax import lax
from jax.experimental import pallas as pl
from jax.experimental.pallas import tpu as pltpu
from jax.sharding import PartitionSpec as P

D = 3584
FFN = 1024
LOC = 448
WIDE = 2 * LOC
EXPERTS = 64
HALF = EXPERTS // 2
TOK = 128
COLD = 8
HOT = 16
MAX_ROWS = EXPERTS * HOT
CR = 128
QR = CR // 4
NC = MAX_ROWS // CR
PAD = 512
PLANE = 16
PLANES = EXPERTS // PLANE
UP_SCALE = D ** -0.5
DOWN_SCALE = FFN ** -0.5
STEP = 4.0
NOISE = 0.25
F32 = jnp.float32
BF16 = jnp.bfloat16


def contract(a, b, da, db):
    return lax.dot_general(a, b, (((da,), (db,)), ((), ())), preferred_element_type=F32)


def stochastic(weights, grads, noise):
    target = weights.astype(F32) - STEP * grads
    return (target + (noise.astype(F32) - 0.5) * (NOISE * jnp.abs(target))).astype(BF16)


def kernel(
    feat, cot, ids_ref, probs_ref, cap_ref, up_hbm, down_hbm, noise_hbm,
    mixed, grad_tok, new_up, new_down,
    fpad, cpad, ids_all, probs_all, pick, phi, plo, packed, xg, ups, dnp, noise, part, r1, r2, r3,
    ad, back, got, half_out, sums,
    load_sem, share_send, share_recv, disp_send, disp_recv, step_send, step_recv, ret_send, ret_recv,
    sum_send, sum_recv,
):
    dp = lax.axis_index("dp")
    me = lax.axis_index("expert")
    plane = me // PLANE
    inplane = lax.rem(me, PLANE)
    hot = me >= HALF
    x = lax.rem(dp, 4)
    z_hi = dp // 4
    bit_a = lax.rem((x + 1) // 2, 2)
    bit_b = x // 2
    peer_a = z_hi * 4 + (x + 1 - 2 * lax.rem(x, 2))
    peer_b = z_hi * 4 + (3 - x)
    peer_z = (1 - z_hi) * 4 + x

    barrier = pltpu.get_barrier_semaphore()

    def other_plane(d):
        return lax.rem(plane + d, PLANES)

    @pl.loop(1, PLANE)
    def _(j):
        pl.semaphore_signal(barrier, inc=1,
                            device_id=(dp, plane * PLANE + lax.rem(inplane + j, PLANE)),
                            device_id_type=pl.DeviceIdType.MESH)

    @pl.loop(1, PLANES)
    def _(d):
        pl.semaphore_signal(barrier, inc=1, device_id=(dp, other_plane(d) * PLANE + inplane),
                            device_id_type=pl.DeviceIdType.MESH)

    for peer in (peer_a, peer_b, peer_z):
        pl.semaphore_signal(barrier, inc=1, device_id=(peer, me),
                            device_id_type=pl.DeviceIdType.MESH)

    loads = [
        pltpu.make_async_copy(up_hbm, ups.at[pl.ds(64, LOC)], load_sem.at[0]),
        pltpu.make_async_copy(down_hbm, dnp.at[pl.ds(0, LOC)], load_sem.at[1]),
        pltpu.make_async_copy(noise_hbm, noise, load_sem.at[2]),
    ]
    for load in loads:
        load.start()

    for p in range(PLANES):
        fpad[p, 0:64, :] = jnp.zeros((64, TOK), BF16)
        cpad[p, LOC:PAD, :] = jnp.zeros((64, TOK), BF16)
    fpad[plane, 64:PAD, :] = feat[...]
    cpad[plane, 0:LOC, :] = cot[...]
    ids_all[plane] = ids_ref[...]
    probs_all[plane] = probs_ref[...]

    def share(d):
        to = other_plane(d)
        pairs = ((ids_ref, ids_all.at[plane]), (probs_ref, probs_all.at[plane]),
                 (cot, cpad.at[plane, pl.ds(0, LOC)]), (feat, fpad.at[plane, pl.ds(64, LOC)]))
        return [pltpu.make_async_remote_copy(
            src_ref=src, dst_ref=dst, send_sem=share_send.at[n, d], recv_sem=share_recv.at[n, d],
            device_id=(dp, to * PLANE + inplane), device_id_type=pl.DeviceIdType.MESH)
            for n, (src, dst) in enumerate(pairs)]

    def source(k):
        return jnp.where(k == 0, plane, jnp.where(
            k == 1, plane + 1 - 2 * lax.rem(plane, 2),
            jnp.where(k == 2, lax.rem(plane + 2, PLANES), 3 - plane)))

    row_e = lax.broadcasted_iota(jnp.int32, (EXPERTS, TOK), 0)
    earlier = jnp.where(
        lax.broadcasted_iota(jnp.int32, (TOK, TOK), 0)
        < lax.broadcasted_iota(jnp.int32, (TOK, TOK), 1), 1.0, 0.0).astype(BF16)
    diagonal = (lax.broadcasted_iota(jnp.int32, (EXPERTS, EXPERTS), 0)
                == lax.broadcasted_iota(jnp.int32, (EXPERTS, EXPERTS), 1))
    limit = jnp.sum(jnp.where(diagonal, cap_ref[...].astype(F32), 0.0), axis=1, keepdims=True)

    def pack(p, count):
        chosen = jnp.zeros((EXPERTS, TOK), F32)
        prob = jnp.zeros((EXPERTS, TOK), F32)
        for k in range(8):
            hit = ids_all[p, k:k + 1, :] == row_e
            chosen = chosen + jnp.where(hit, 1.0, 0.0)
            prob = prob + jnp.where(hit, probs_all[p, k:k + 1, :], 0.0)
        rank = jnp.dot(chosen.astype(BF16), earlier, preferred_element_type=F32)
        kept = jnp.where((chosen > 0.5) & (rank < limit), rank, -1.0).astype(BF16)
        prob_hi = prob.astype(BF16)
        prob_lo = (prob - prob_hi.astype(F32)).astype(BF16)
        for i in range(PLANE * count // TOK):
            rows = pl.ds(i * TOK, TOK)
            r_e = lax.broadcasted_iota(jnp.int32, (TOK, EXPERTS), 0) + i * TOK
            lane_e = lax.broadcasted_iota(jnp.int32, (TOK, EXPERTS), 1)
            slot_of = lax.rem(lax.broadcasted_iota(jnp.int32, (TOK, TOK), 0), count)
            spread = jnp.where(r_e // count + plane * PLANE == lane_e, 1.0, 0.0).astype(BF16)
            match = contract(spread, kept, 1, 0) == slot_of.astype(F32)
            sel = jnp.where(match, 1.0, 0.0).astype(BF16)
            w_hi = jnp.where(match, contract(spread, prob_hi, 1, 0), 0.0).astype(BF16)
            w_lo = jnp.where(match, contract(spread, prob_lo, 1, 0), 0.0).astype(BF16)
            pick[p, rows, :] = sel
            phi[p, rows, :] = w_hi
            plo[p, rows, :] = w_lo
            g = contract(w_hi, cpad[p], 1, 1) + contract(w_lo, cpad[p], 1, 1)
            f = contract(sel, fpad[p], 1, 1)
            packed[p, rows, 0:384] = g[:, 0:384].astype(BF16)
            packed[p, rows, 384:512] = (g[:, 384:512] + f[:, 0:128]).astype(BF16)
            packed[p, rows, 512:WIDE] = f[:, 128:512].astype(BF16)

    def send_block(p, count):
        block = p * PLANE + inplane

        @pl.loop(0, PLANE)
        def _(j):
            place = lax.rem(inplane + j, PLANE)
            src = packed.at[p, pl.ds(pl.multiple_of(place * count, 8), count)]
            dst = xg.at[pl.ds(pl.multiple_of(block * count, 8), count)]
            sem = disp_recv.at[(block * count) // CR]

            @pl.when(place != inplane)
            def _():
                pltpu.make_async_remote_copy(
                    src_ref=src, dst_ref=dst, send_sem=disp_send, recv_sem=sem,
                    device_id=(dp, plane * PLANE + place),
                    device_id_type=pl.DeviceIdType.MESH).start()

            @pl.when(place == inplane)
            def _():
                pltpu.make_async_copy(src, dst, sem).start()

    def by_kind(work, *operands):
        @pl.when(hot)
        def _():
            work(*operands, HOT)

        @pl.when(jnp.logical_not(hot))
        def _():
            work(*operands, COLD)

    by_kind(pack, plane)
    pl.semaphore_wait(barrier, PLANE - 1 + PLANES - 1 + 3)
    by_kind(send_block, plane)
    for k in range(1, PLANES):
        for copy in share(lax.rem(source(k) - plane + PLANES, PLANES)):
            copy.start()

    def pack_next(i):
        @pl.when(i < PLANES - 1)
        def _():
            p = source(i + 1)
            d = lax.rem(plane - p + PLANES, PLANES)
            for copy in share(d):
                copy.wait_recv()
            by_kind(pack, p)
            by_kind(send_block, p)

    ups[0:64, :] = jnp.zeros((64, FFN), BF16)
    dnp[LOC:PAD, :] = jnp.zeros((64, FFN), BF16)
    for load in loads:
        load.wait()

    def remote(src, dst, stage, c, w, peer):
        return lambda: pltpu.make_async_remote_copy(
            src_ref=src, dst_ref=dst, send_sem=step_send.at[stage, c, w],
            recv_sem=step_recv.at[stage, c, w], device_id=(peer, me),
            device_id_type=pl.DeviceIdType.MESH)

    def copies(stage, c):
        if stage == 0:
            return [remote(part.at[c, 0, 1 - bit_a], r1.at[c, 0], 0, c, 0, peer_a),
                    remote(part.at[c, 1, :, 1 - bit_b], r1.at[c, 1], 0, c, 1, peer_b)]
        if stage == 1:
            return [remote(r1.at[c, 0, 1 - bit_b], r2.at[c, 0], 1, c, 0, peer_b),
                    remote(r1.at[c, 1, 1 - bit_a], r2.at[c, 1], 1, c, 1, peer_a)]
        if stage == 2:
            return [remote(r2.at[c], r3.at[c], 2, c, 0, peer_z)]
        if stage == 3:
            q0, q1 = ad.at[0, c, bit_a, bit_b], ad.at[1, c, bit_a, bit_b]
            return [remote(q0, q0, 3, c, 0, peer_b), remote(q1, q1, 3, c, 1, peer_a)]
        h0, h1 = ad.at[0, c, bit_a], ad.at[1, c, :, bit_b]
        return [remote(h0, h0, 4, c, 0, peer_a), remote(h1, h1, 4, c, 1, peer_b)]

    def start(stage, c):
        for copy in copies(stage, c):
            copy().start()

    def start_one(stage, c, w):
        copies(stage, c)[w]().start()

    def arrived(stage, c):
        for copy in copies(stage, c):
            copy().wait_recv()

    def arrived_one(stage, c, w):
        copies(stage, c)[w]().wait_recv()

    def add(u, v):
        return (u.astype(F32) + v.astype(F32)).astype(BF16)

    chunks = jnp.where(hot, NC, NC // 2)

    def chunk_at(i):
        return jnp.where(hot, source(i // 2) * 2 + lax.rem(i, 2), source(i))

    def products_in(i):
        c = chunk_at(i)
        rows = pl.ds(pl.multiple_of(c * CR, CR), CR)
        pltpu.make_async_copy(xg.at[rows], xg.at[rows], disp_recv.at[c]).wait()
        shape = (2, 2, QR, FFN)
        pre = contract(xg[rows, 384:WIDE], ups[...], 1, 0) * UP_SCALE
        part[c, 0] = pre.astype(BF16).reshape(shape)
        start_one(0, c, 0)
        dact = contract(xg[rows, 0:PAD], dnp[...], 1, 0) * DOWN_SCALE
        part[c, 1] = dact.astype(BF16).reshape(shape)
        start_one(0, c, 1)

    def add_first(i):
        c = chunk_at(i)
        arrived_one(0, c, 0)
        r1[c, 0] = add(r1[c, 0], part[c, 0, bit_a])
        start_one(1, c, 0)
        arrived_one(0, c, 1)
        for a in range(2):
            r1[c, 1, a] = add(r1[c, 1, a], part[c, 1, a, bit_b])
        start_one(1, c, 1)

    def add_second(i):
        c = chunk_at(i)
        arrived(1, c)
        r2[c, 0] = add(r2[c, 0], r1[c, 0, bit_b])
        r2[c, 1] = add(r2[c, 1], r1[c, 1, bit_a])
        start(2, c)

    def activate(i):
        c = chunk_at(i)
        arrived(2, c)
        pre = r3[c, 0].astype(F32) + r2[c, 0].astype(F32)
        dact = r3[c, 1].astype(F32) + r2[c, 1].astype(F32)
        s = 1.0 / (1.0 + jnp.exp(-pre))
        ad[0, c, bit_a, bit_b] = (pre * s).astype(BF16)
        ad[1, c, bit_a, bit_b] = (dact * (s * (1.0 + pre * (1.0 - s)))).astype(BF16)
        start(3, c)

    def pass_half(i):
        c = chunk_at(i)
        for w in range(2):
            arrived_one(3, c, w)
            start_one(4, c, w)

    def send_back(c, count):
        per = CR // count

        @pl.loop(0, per)
        def _(j):
            block = c * per + j
            p, place = block // PLANE, lax.rem(block, PLANE)
            src = back.at[pl.ds(pl.multiple_of(block * count, 8), count)]
            dst = got.at[p, pl.ds(pl.multiple_of(inplane * count, 8), count)]

            @pl.when(place != inplane)
            def _():
                pltpu.make_async_remote_copy(
                    src_ref=src, dst_ref=dst, send_sem=ret_send, recv_sem=ret_recv.at[p],
                    device_id=(dp, plane * PLANE + place),
                    device_id_type=pl.DeviceIdType.MESH).start()

            @pl.when(place == inplane)
            def _():
                pltpu.make_async_copy(src, dst, ret_recv.at[p]).start()

    def products_out(i):
        c = chunk_at(i)
        arrived(4, c)
        base = c * CR
        rows = pl.ds(pl.multiple_of(base, CR), CR)
        y = contract(ad[0, c].reshape(CR, FFN), dnp[...], 1, 1) * DOWN_SCALE
        d = contract(ad[1, c].reshape(CR, FFN), ups[...], 1, 1) * UP_SCALE
        back[rows, 0:384] = y[:, 0:384].astype(BF16)
        back[rows, 384:512] = (y[:, 384:512] + d[:, 0:128]).astype(BF16)
        back[rows, 512:WIDE] = d[:, 128:512].astype(BF16)

        @pl.when(hot)
        def _():
            send_back(c, HOT)

        @pl.when(jnp.logical_not(hot))
        def _():
            send_back(c, COLD)

    def total_copy(d):
        to = other_plane(d)
        return pltpu.make_async_remote_copy(
            src_ref=half_out.at[to], dst_ref=sums.at[plane], send_sem=sum_send.at[d],
            recv_sem=sum_recv.at[d], device_id=(dp, to * PLANE + inplane),
            device_id_type=pl.DeviceIdType.MESH)

    def combine(p, count):
        n = PLANE * count
        rows = got.at[p, pl.ds(0, n)]
        pltpu.make_async_copy(rows, rows, ret_recv.at[p]).wait()
        out = got[p, 0:n, 0:PAD]
        m = contract(out, phi[p, 0:n, :], 0, 0) + contract(out, plo[p, 0:n, :], 0, 0)
        half_out[p, 0] = m[0:LOC, :].astype(BF16)
        g = contract(got[p, 0:n, 384:WIDE], pick[p, 0:n, :], 0, 0)
        half_out[p, 1] = g[64:PAD, :].astype(BF16)

        @pl.when(p != plane)
        def _():
            total_copy(lax.rem(p - plane + PLANES, PLANES)).start()

    def combine_next(i):
        @pl.when(hot & (lax.rem(i, 2) == 1))
        def _():
            combine(source(i // 2), HOT)

        @pl.when(jnp.logical_not(hot))
        def _():
            combine(source(i), COLD)

    schedule = [
        (add_first, 1), (activate, 2), (products_in, 0), (add_second, 1), (products_out, 3),
        (pass_half, 2), (pack_next, 0), (combine_next, 4),
    ]
    lag_max = 3

    @pl.loop(0, chunks + lag_max)
    def _(t):
        for stage, lag in schedule:
            i = t - lag

            @pl.when((i >= 0) & (i < chunks))
            def _(stage=stage, i=i):
                stage(i)

    def update_up(slots):
        count = EXPERTS * slots
        dpre = ad[1, 0:count // CR].reshape(count, FFN)
        for lo in range(0, PAD, 128):
            hi = lo + 128
            grad = contract(xg[0:count, 384 + lo:384 + hi], dpre, 0, 0)
            skip = 64 if lo == 0 else 0
            new_up[lo + skip - 64:hi - 64, :] = stochastic(
                ups[lo + skip:hi, :], UP_SCALE * grad[skip:, :], noise[lo + skip - 64:hi - 64, :])

    def update_down(slots):
        count = EXPERTS * slots
        act = ad[0, 0:count // CR].reshape(count, FFN)
        for lo in range(0, PAD, 128):
            grad = contract(xg[0:count, lo:lo + 128], act, 0, 0)
            hi = min(lo + 128, LOC)
            new_down[lo:hi, :] = stochastic(
                dnp[lo:hi, :], DOWN_SCALE * grad[0:hi - lo, :], noise[lo:hi, :])

    by_kind(update_up)
    combine_next(chunks - 1)
    by_kind(update_down)

    m = half_out[plane, 0].astype(F32)
    g = half_out[plane, 1].astype(F32)
    for d in range(1, PLANES):
        total_copy(d).wait_recv()
        p = lax.rem(plane - d + PLANES, PLANES)
        m = m + sums[p, 0].astype(F32)
        g = g + sums[p, 1].astype(F32)
    mixed[...] = m.astype(BF16)
    grad_tok[...] = g.astype(BF16)

    @pl.loop(0, chunks)
    def _(c):
        for stage in range(5):
            for copy in copies(stage, c):
                copy().wait_send()

    for d in range(1, PLANES):
        total_copy(d).wait_send()
        for copy in share(d):
            copy.wait_send()

    def drain(count):
        sent = back.at[pl.ds(0, PLANES * (PLANE - 1) * count)]
        pltpu.make_async_copy(sent, sent, disp_send).wait()
        pltpu.make_async_copy(sent, sent, ret_send).wait()

    @pl.when(hot)
    def _():
        drain(HOT)

    @pl.when(jnp.logical_not(hot))
    def _():
        drain(COLD)


def shards(
    features, upstream, expert_ids, gate_probs, capacity, up_weight, down_weight, round_noise
):
    vmem = pl.BlockSpec(memory_space=pltpu.VMEM)
    hbm = pl.BlockSpec(memory_space=pl.ANY)
    shape = jax.ShapeDtypeStruct
    mixed, grad_tok, new_up, new_down = pl.pallas_call(
        kernel,
        out_shape=(
            shape((LOC, TOK), BF16), shape((LOC, TOK), BF16),
            shape((LOC, FFN), BF16), shape((LOC, FFN), BF16),
        ),
        in_specs=[vmem] * 5 + [hbm] * 3,
        out_specs=(vmem,) * 4,
        scratch_shapes=[
            pltpu.VMEM((PLANES, PAD, TOK), BF16),
            pltpu.VMEM((PLANES, PAD, TOK), BF16),
            pltpu.VMEM((PLANES, 8, TOK), jnp.int32),
            pltpu.VMEM((PLANES, 8, TOK), F32),
            pltpu.VMEM((PLANES, PLANE * HOT, TOK), BF16),
            pltpu.VMEM((PLANES, PLANE * HOT, TOK), BF16),
            pltpu.VMEM((PLANES, PLANE * HOT, TOK), BF16),
            pltpu.VMEM((PLANES, PLANE * HOT, WIDE), BF16),
            pltpu.VMEM((MAX_ROWS, WIDE), BF16),
            pltpu.VMEM((PAD, FFN), BF16),
            pltpu.VMEM((PAD, FFN), BF16),
            pltpu.VMEM((LOC, FFN), BF16),
            pltpu.VMEM((NC, 2, 2, 2, QR, FFN), BF16),
            pltpu.VMEM((NC, 2, 2, QR, FFN), BF16),
            pltpu.VMEM((NC, 2, QR, FFN), BF16),
            pltpu.VMEM((NC, 2, QR, FFN), BF16),
            pltpu.VMEM((2, NC, 2, 2, QR, FFN), BF16),
            pltpu.VMEM((MAX_ROWS, WIDE), BF16),
            pltpu.VMEM((PLANES, PLANE * HOT, WIDE), BF16),
            pltpu.VMEM((PLANES, 2, LOC, TOK), BF16),
            pltpu.VMEM((PLANES, 2, LOC, TOK), BF16),
            pltpu.SemaphoreType.DMA((3,)),
            pltpu.SemaphoreType.DMA((4, PLANES)),
            pltpu.SemaphoreType.DMA((4, PLANES)),
            pltpu.SemaphoreType.DMA,
            pltpu.SemaphoreType.DMA((NC,)),
            pltpu.SemaphoreType.DMA((5, NC, 2)),
            pltpu.SemaphoreType.DMA((5, NC, 2)),
            pltpu.SemaphoreType.DMA,
            pltpu.SemaphoreType.DMA((PLANES,)),
            pltpu.SemaphoreType.DMA((PLANES,)),
            pltpu.SemaphoreType.DMA((PLANES,)),
        ],
        compiler_params=pltpu.CompilerParams(
            collective_id=0, has_side_effects=True, vmem_limit_bytes=56 * 1024 * 1024),
    )(features.T, upstream.T, expert_ids.T, gate_probs.T, capacity.reshape(1, EXPERTS),
      up_weight[0], down_weight[0].T, round_noise[0])
    return mixed.T, grad_tok.T, new_up[None], new_down.T[None]


def solution(mesh):
    in_specs = (
        P("expert", "dp"),
        P("expert", "dp"),
        P("expert", None),
        P("expert", None),
        P(),
        P("expert", "dp", None),
        P("expert", None, "dp"),
        P("expert", "dp", None),
    )
    out_specs = (
        P("expert", "dp"),
        P("expert", "dp"),
        P("expert", "dp", None),
        P("expert", None, "dp"),
    )
    return jax.shard_map(shards, mesh=mesh, in_specs=in_specs, out_specs=out_specs, check_vma=False)
```

```python
import jax
import jax.numpy as jnp
from jax import lax
from jax.experimental import pallas as pl
from jax.experimental.pallas import tpu as pltpu
from jax.sharding import PartitionSpec as P

D = 3584
FFN = 1024
LOC = 448
WIDE = 2 * LOC
EXPERTS = 64
HALF = EXPERTS // 2
TOK = 128
COLD = 8
HOT = 16
MAX_ROWS = EXPERTS * HOT
CR = 128
QR = CR // 4
NC = MAX_ROWS // CR
PAD = 512
PLANE = 16
PLANES = EXPERTS // PLANE
UP_SCALE = D ** -0.5
DOWN_SCALE = FFN ** -0.5
STEP = 4.0
NOISE = 0.25
F32 = jnp.float32
BF16 = jnp.bfloat16


def contract(a, b, da, db):
    return lax.dot_general(a, b, (((da,), (db,)), ((), ())), preferred_element_type=F32)


def stochastic(weights, grads, noise):
    target = weights.astype(F32) - STEP * grads
    return (target + (noise.astype(F32) - 0.5) * (NOISE * jnp.abs(target))).astype(BF16)


def kernel(
    feat, cot, ids_ref, probs_ref, cap_ref, up_hbm, down_hbm, noise_hbm,
    mixed, grad_tok, new_up, new_down,
    fpad, cpad, ids_all, probs_all, pick, phi, plo, packed, xg, ups, dnp, noise, part, r1, r2, r3,
    ad, back, got, half_out, sums,
    load_sem, share_send, share_recv, disp_send, disp_recv, step_send, step_recv, ret_send, ret_recv,
    sum_send, sum_recv,
):
    dp = lax.axis_index("dp")
    me = lax.axis_index("expert")
    plane = me // PLANE
    inplane = lax.rem(me, PLANE)
    hot = me >= HALF
    x = lax.rem(dp, 4)
    z_hi = dp // 4
    bit_a = lax.rem((x + 1) // 2, 2)
    bit_b = x // 2
    peer_a = z_hi * 4 + (x + 1 - 2 * lax.rem(x, 2))
    peer_b = z_hi * 4 + (3 - x)
    peer_z = (1 - z_hi) * 4 + x

    barrier = pltpu.get_barrier_semaphore()

    def other_plane(d):
        return lax.rem(plane + d, PLANES)

    @pl.loop(1, PLANE)
    def _(j):
        pl.semaphore_signal(barrier, inc=1,
                            device_id=(dp, plane * PLANE + lax.rem(inplane + j, PLANE)),
                            device_id_type=pl.DeviceIdType.MESH)

    @pl.loop(1, PLANES)
    def _(d):
        pl.semaphore_signal(barrier, inc=1, device_id=(dp, other_plane(d) * PLANE + inplane),
                            device_id_type=pl.DeviceIdType.MESH)

    for peer in (peer_a, peer_b, peer_z):
        pl.semaphore_signal(barrier, inc=1, device_id=(peer, me),
                            device_id_type=pl.DeviceIdType.MESH)

    loads = [
        pltpu.make_async_copy(up_hbm, ups.at[pl.ds(64, LOC)], load_sem.at[0]),
        pltpu.make_async_copy(down_hbm, dnp.at[pl.ds(0, LOC)], load_sem.at[1]),
        pltpu.make_async_copy(noise_hbm, noise, load_sem.at[2]),
    ]
    for load in loads:
        load.start()

    for p in range(PLANES):
        fpad[p, 0:64, :] = jnp.zeros((64, TOK), BF16)
        cpad[p, LOC:PAD, :] = jnp.zeros((64, TOK), BF16)
    fpad[plane, 64:PAD, :] = feat[...]
    cpad[plane, 0:LOC, :] = cot[...]
    ids_all[plane] = ids_ref[...]
    probs_all[plane] = probs_ref[...]

    def share(d):
        to = other_plane(d)
        pairs = ((ids_ref, ids_all.at[plane]), (probs_ref, probs_all.at[plane]),
                 (cot, cpad.at[plane, pl.ds(0, LOC)]), (feat, fpad.at[plane, pl.ds(64, LOC)]))
        return [pltpu.make_async_remote_copy(
            src_ref=src, dst_ref=dst, send_sem=share_send.at[n, d], recv_sem=share_recv.at[n, d],
            device_id=(dp, to * PLANE + inplane), device_id_type=pl.DeviceIdType.MESH)
            for n, (src, dst) in enumerate(pairs)]

    def source(k):
        return jnp.where(k == 0, plane, jnp.where(
            k == 1, plane + 1 - 2 * lax.rem(plane, 2),
            jnp.where(k == 2, lax.rem(plane + 2, PLANES), 3 - plane)))

    row_e = lax.broadcasted_iota(jnp.int32, (EXPERTS, TOK), 0)
    earlier = jnp.where(
        lax.broadcasted_iota(jnp.int32, (TOK, TOK), 0)
        < lax.broadcasted_iota(jnp.int32, (TOK, TOK), 1), 1.0, 0.0).astype(BF16)
    diagonal = (lax.broadcasted_iota(jnp.int32, (EXPERTS, EXPERTS), 0)
                == lax.broadcasted_iota(jnp.int32, (EXPERTS, EXPERTS), 1))
    limit = jnp.sum(jnp.where(diagonal, cap_ref[...].astype(F32), 0.0), axis=1, keepdims=True)

    def pack(p, count):
        chosen = jnp.zeros((EXPERTS, TOK), F32)
        prob = jnp.zeros((EXPERTS, TOK), F32)
        for k in range(8):
            hit = ids_all[p, k:k + 1, :] == row_e
            chosen = chosen + jnp.where(hit, 1.0, 0.0)
            prob = prob + jnp.where(hit, probs_all[p, k:k + 1, :], 0.0)
        rank = jnp.dot(chosen.astype(BF16), earlier, preferred_element_type=F32)
        kept = jnp.where((chosen > 0.5) & (rank < limit), rank, -1.0).astype(BF16)
        prob_hi = prob.astype(BF16)
        prob_lo = (prob - prob_hi.astype(F32)).astype(BF16)
        for i in range(PLANE * count // TOK):
            rows = pl.ds(i * TOK, TOK)
            r_e = lax.broadcasted_iota(jnp.int32, (TOK, EXPERTS), 0) + i * TOK
            lane_e = lax.broadcasted_iota(jnp.int32, (TOK, EXPERTS), 1)
            slot_of = lax.rem(lax.broadcasted_iota(jnp.int32, (TOK, TOK), 0), count)
            spread = jnp.where(r_e // count + plane * PLANE == lane_e, 1.0, 0.0).astype(BF16)
            match = contract(spread, kept, 1, 0) == slot_of.astype(F32)
            sel = jnp.where(match, 1.0, 0.0).astype(BF16)
            w_hi = jnp.where(match, contract(spread, prob_hi, 1, 0), 0.0).astype(BF16)
            w_lo = jnp.where(match, contract(spread, prob_lo, 1, 0), 0.0).astype(BF16)
            pick[p, rows, :] = sel
            phi[p, rows, :] = w_hi
            plo[p, rows, :] = w_lo
            g = contract(w_hi, cpad[p], 1, 1) + contract(w_lo, cpad[p], 1, 1)
            f = contract(sel, fpad[p], 1, 1)
            packed[p, rows, 0:384] = g[:, 0:384].astype(BF16)
            packed[p, rows, 384:512] = (g[:, 384:512] + f[:, 0:128]).astype(BF16)
            packed[p, rows, 512:WIDE] = f[:, 128:512].astype(BF16)

    def send_block(p, count):
        block = p * PLANE + inplane

        @pl.loop(0, PLANE)
        def _(j):
            place = lax.rem(inplane + j, PLANE)
            src = packed.at[p, pl.ds(pl.multiple_of(place * count, 8), count)]
            dst = xg.at[pl.ds(pl.multiple_of(block * count, 8), count)]
            sem = disp_recv.at[(block * count) // CR]

            @pl.when(place != inplane)
            def _():
                pltpu.make_async_remote_copy(
                    src_ref=src, dst_ref=dst, send_sem=disp_send, recv_sem=sem,
                    device_id=(dp, plane * PLANE + place),
                    device_id_type=pl.DeviceIdType.MESH).start()

            @pl.when(place == inplane)
            def _():
                pltpu.make_async_copy(src, dst, sem).start()

    def by_kind(work, *operands):
        @pl.when(hot)
        def _():
            work(*operands, HOT)

        @pl.when(jnp.logical_not(hot))
        def _():
            work(*operands, COLD)

    by_kind(pack, plane)
    pl.semaphore_wait(barrier, PLANE - 1 + PLANES - 1 + 3)
    by_kind(send_block, plane)
    for k in range(1, PLANES):
        for copy in share(lax.rem(source(k) - plane + PLANES, PLANES)):
            copy.start()

    def pack_next(i):
        @pl.when(i < PLANES - 1)
        def _():
            p = source(i + 1)
            d = lax.rem(plane - p + PLANES, PLANES)
            for copy in share(d):
                copy.wait_recv()
            by_kind(pack, p)
            by_kind(send_block, p)

    ups[0:64, :] = jnp.zeros((64, FFN), BF16)
    dnp[LOC:PAD, :] = jnp.zeros((64, FFN), BF16)
    for load in loads:
        load.wait()

    def remote(src, dst, stage, c, w, peer):
        return lambda: pltpu.make_async_remote_copy(
            src_ref=src, dst_ref=dst, send_sem=step_send.at[stage, c, w],
            recv_sem=step_recv.at[stage, c, w], device_id=(peer, me),
            device_id_type=pl.DeviceIdType.MESH)

    def copies(stage, c):
        if stage == 0:
            return [remote(part.at[c, 0, 1 - bit_a], r1.at[c, 0], 0, c, 0, peer_a),
                    remote(part.at[c, 1, :, 1 - bit_b], r1.at[c, 1], 0, c, 1, peer_b)]
        if stage == 1:
            return [remote(r1.at[c, 0, 1 - bit_b], r2.at[c, 0], 1, c, 0, peer_b),
                    remote(r1.at[c, 1, 1 - bit_a], r2.at[c, 1], 1, c, 1, peer_a)]
        if stage == 2:
            return [remote(r2.at[c], r3.at[c], 2, c, 0, peer_z)]
        if stage == 3:
            q0, q1 = ad.at[0, c, bit_a, bit_b], ad.at[1, c, bit_a, bit_b]
            return [remote(q0, q0, 3, c, 0, peer_b), remote(q1, q1, 3, c, 1, peer_a)]
        h0, h1 = ad.at[0, c, bit_a], ad.at[1, c, :, bit_b]
        return [remote(h0, h0, 4, c, 0, peer_a), remote(h1, h1, 4, c, 1, peer_b)]

    def start(stage, c):
        for copy in copies(stage, c):
            copy().start()

    def start_one(stage, c, w):
        copies(stage, c)[w]().start()

    def arrived(stage, c):
        for copy in copies(stage, c):
            copy().wait_recv()

    def arrived_one(stage, c, w):
        copies(stage, c)[w]().wait_recv()

    def add(u, v):
        return (u.astype(F32) + v.astype(F32)).astype(BF16)

    chunks = jnp.where(hot, NC, NC // 2)

    def chunk_at(i):
        return jnp.where(hot, source(i // 2) * 2 + lax.rem(i, 2), source(i))

    def products_in(i):
        c = chunk_at(i)
        rows = pl.ds(pl.multiple_of(c * CR, CR), CR)
        pltpu.make_async_copy(xg.at[rows], xg.at[rows], disp_recv.at[c]).wait()
        shape = (2, 2, QR, FFN)
        pre = contract(xg[rows, 384:WIDE], ups[...], 1, 0) * UP_SCALE
        part[c, 0] = pre.astype(BF16).reshape(shape)
        start_one(0, c, 0)
        dact = contract(xg[rows, 0:PAD], dnp[...], 1, 0) * DOWN_SCALE
        part[c, 1] = dact.astype(BF16).reshape(shape)
        start_one(0, c, 1)

    def add_first(i):
        c = chunk_at(i)
        arrived_one(0, c, 0)
        r1[c, 0] = add(r1[c, 0], part[c, 0, bit_a])
        start_one(1, c, 0)
        arrived_one(0, c, 1)
        for a in range(2):
            r1[c, 1, a] = add(r1[c, 1, a], part[c, 1, a, bit_b])
        start_one(1, c, 1)

    def add_second(i):
        c = chunk_at(i)
        arrived(1, c)
        r2[c, 0] = add(r2[c, 0], r1[c, 0, bit_b])
        r2[c, 1] = add(r2[c, 1], r1[c, 1, bit_a])
        start(2, c)

    def activate(i):
        c = chunk_at(i)
        arrived(2, c)
        pre = r3[c, 0].astype(F32) + r2[c, 0].astype(F32)
        dact = r3[c, 1].astype(F32) + r2[c, 1].astype(F32)
        s = 1.0 / (1.0 + jnp.exp(-pre))
        ad[0, c, bit_a, bit_b] = (pre * s).astype(BF16)
        start_one(3, c, 0)
        ad[1, c, bit_a, bit_b] = (dact * (s * (1.0 + pre * (1.0 - s)))).astype(BF16)
        start_one(3, c, 1)

    def pass_half(i):
        c = chunk_at(i)
        for w in range(2):
            arrived_one(3, c, w)
            start_one(4, c, w)

    def send_back(c, count):
        per = CR // count

        @pl.loop(0, per)
        def _(j):
            block = c * per + j
            p, place = block // PLANE, lax.rem(block, PLANE)
            src = back.at[pl.ds(pl.multiple_of(block * count, 8), count)]
            dst = got.at[p, pl.ds(pl.multiple_of(inplane * count, 8), count)]

            @pl.when(place != inplane)
            def _():
                pltpu.make_async_remote_copy(
                    src_ref=src, dst_ref=dst, send_sem=ret_send, recv_sem=ret_recv.at[p],
                    device_id=(dp, plane * PLANE + place),
                    device_id_type=pl.DeviceIdType.MESH).start()

            @pl.when(place == inplane)
            def _():
                pltpu.make_async_copy(src, dst, ret_recv.at[p]).start()

    def products_out(i):
        c = chunk_at(i)
        arrived(4, c)
        base = c * CR
        rows = pl.ds(pl.multiple_of(base, CR), CR)
        y = contract(ad[0, c].reshape(CR, FFN), dnp[...], 1, 1) * DOWN_SCALE
        d = contract(ad[1, c].reshape(CR, FFN), ups[...], 1, 1) * UP_SCALE
        back[rows, 0:384] = y[:, 0:384].astype(BF16)
        back[rows, 384:512] = (y[:, 384:512] + d[:, 0:128]).astype(BF16)
        back[rows, 512:WIDE] = d[:, 128:512].astype(BF16)

        @pl.when(hot)
        def _():
            send_back(c, HOT)

        @pl.when(jnp.logical_not(hot))
        def _():
            send_back(c, COLD)

    def total_copy(d):
        to = other_plane(d)
        return pltpu.make_async_remote_copy(
            src_ref=half_out.at[to], dst_ref=sums.at[plane], send_sem=sum_send.at[d],
            recv_sem=sum_recv.at[d], device_id=(dp, to * PLANE + inplane),
            device_id_type=pl.DeviceIdType.MESH)

    def combine(p, count):
        n = PLANE * count
        rows = got.at[p, pl.ds(0, n)]
        pltpu.make_async_copy(rows, rows, ret_recv.at[p]).wait()
        out = got[p, 0:n, 0:PAD]
        m = contract(out, phi[p, 0:n, :], 0, 0) + contract(out, plo[p, 0:n, :], 0, 0)
        half_out[p, 0] = m[0:LOC, :].astype(BF16)
        g = contract(got[p, 0:n, 384:WIDE], pick[p, 0:n, :], 0, 0)
        half_out[p, 1] = g[64:PAD, :].astype(BF16)

        @pl.when(p != plane)
        def _():
            total_copy(lax.rem(p - plane + PLANES, PLANES)).start()

    def combine_next(i):
        @pl.when(hot & (lax.rem(i, 2) == 1))
        def _():
            combine(source(i // 2), HOT)

        @pl.when(jnp.logical_not(hot))
        def _():
            combine(source(i), COLD)

    schedule = [
        (add_first, 1), (activate, 2), (products_in, 0), (add_second, 1), (products_out, 3),
        (pass_half, 2), (pack_next, 0), (combine_next, 4),
    ]
    lag_max = 3

    @pl.loop(0, chunks + lag_max)
    def _(t):
        for stage, lag in schedule:
            i = t - lag

            @pl.when((i >= 0) & (i < chunks))
            def _(stage=stage, i=i):
                stage(i)

    def update_up(slots):
        count = EXPERTS * slots
        dpre = ad[1, 0:count // CR].reshape(count, FFN)
        for lo in range(0, PAD, 128):
            hi = lo + 128
            grad = contract(xg[0:count, 384 + lo:384 + hi], dpre, 0, 0)
            skip = 64 if lo == 0 else 0
            new_up[lo + skip - 64:hi - 64, :] = stochastic(
                ups[lo + skip:hi, :], UP_SCALE * grad[skip:, :], noise[lo + skip - 64:hi - 64, :])

    def update_down(slots):
        count = EXPERTS * slots
        act = ad[0, 0:count // CR].reshape(count, FFN)
        for lo in range(0, PAD, 128):
            grad = contract(xg[0:count, lo:lo + 128], act, 0, 0)
            hi = min(lo + 128, LOC)
            new_down[lo:hi, :] = stochastic(
                dnp[lo:hi, :], DOWN_SCALE * grad[0:hi - lo, :], noise[lo:hi, :])

    by_kind(update_up)
    combine_next(chunks - 1)
    by_kind(update_down)

    m = half_out[plane, 0].astype(F32)
    g = half_out[plane, 1].astype(F32)
    for d in range(1, PLANES):
        total_copy(d).wait_recv()
        p = lax.rem(plane - d + PLANES, PLANES)
        m = m + sums[p, 0].astype(F32)
        g = g + sums[p, 1].astype(F32)
    mixed[...] = m.astype(BF16)
    grad_tok[...] = g.astype(BF16)

    @pl.loop(0, chunks)
    def _(c):
        for stage in range(5):
            for copy in copies(stage, c):
                copy().wait_send()

    for d in range(1, PLANES):
        total_copy(d).wait_send()
        for copy in share(d):
            copy.wait_send()

    def drain(count):
        sent = back.at[pl.ds(0, PLANES * (PLANE - 1) * count)]
        pltpu.make_async_copy(sent, sent, disp_send).wait()
        pltpu.make_async_copy(sent, sent, ret_send).wait()

    @pl.when(hot)
    def _():
        drain(HOT)

    @pl.when(jnp.logical_not(hot))
    def _():
        drain(COLD)


def shards(
    features, upstream, expert_ids, gate_probs, capacity, up_weight, down_weight, round_noise
):
    vmem = pl.BlockSpec(memory_space=pltpu.VMEM)
    hbm = pl.BlockSpec(memory_space=pl.ANY)
    shape = jax.ShapeDtypeStruct
    mixed, grad_tok, new_up, new_down = pl.pallas_call(
        kernel,
        out_shape=(
            shape((LOC, TOK), BF16), shape((LOC, TOK), BF16),
            shape((LOC, FFN), BF16), shape((LOC, FFN), BF16),
        ),
        in_specs=[vmem] * 5 + [hbm] * 3,
        out_specs=(vmem,) * 4,
        scratch_shapes=[
            pltpu.VMEM((PLANES, PAD, TOK), BF16),
            pltpu.VMEM((PLANES, PAD, TOK), BF16),
            pltpu.VMEM((PLANES, 8, TOK), jnp.int32),
            pltpu.VMEM((PLANES, 8, TOK), F32),
            pltpu.VMEM((PLANES, PLANE * HOT, TOK), BF16),
            pltpu.VMEM((PLANES, PLANE * HOT, TOK), BF16),
            pltpu.VMEM((PLANES, PLANE * HOT, TOK), BF16),
            pltpu.VMEM((PLANES, PLANE * HOT, WIDE), BF16),
            pltpu.VMEM((MAX_ROWS, WIDE), BF16),
            pltpu.VMEM((PAD, FFN), BF16),
            pltpu.VMEM((PAD, FFN), BF16),
            pltpu.VMEM((LOC, FFN), BF16),
            pltpu.VMEM((NC, 2, 2, 2, QR, FFN), BF16),
            pltpu.VMEM((NC, 2, 2, QR, FFN), BF16),
            pltpu.VMEM((NC, 2, QR, FFN), BF16),
            pltpu.VMEM((NC, 2, QR, FFN), BF16),
            pltpu.VMEM((2, NC, 2, 2, QR, FFN), BF16),
            pltpu.VMEM((MAX_ROWS, WIDE), BF16),
            pltpu.VMEM((PLANES, PLANE * HOT, WIDE), BF16),
            pltpu.VMEM((PLANES, 2, LOC, TOK), BF16),
            pltpu.VMEM((PLANES, 2, LOC, TOK), BF16),
            pltpu.SemaphoreType.DMA((3,)),
            pltpu.SemaphoreType.DMA((4, PLANES)),
            pltpu.SemaphoreType.DMA((4, PLANES)),
            pltpu.SemaphoreType.DMA,
            pltpu.SemaphoreType.DMA((NC,)),
            pltpu.SemaphoreType.DMA((5, NC, 2)),
            pltpu.SemaphoreType.DMA((5, NC, 2)),
            pltpu.SemaphoreType.DMA,
            pltpu.SemaphoreType.DMA((PLANES,)),
            pltpu.SemaphoreType.DMA((PLANES,)),
            pltpu.SemaphoreType.DMA((PLANES,)),
        ],
        compiler_params=pltpu.CompilerParams(
            collective_id=0, has_side_effects=True, vmem_limit_bytes=56 * 1024 * 1024),
    )(features.T, upstream.T, expert_ids.T, gate_probs.T, capacity.reshape(1, EXPERTS),
      up_weight[0], down_weight[0].T, round_noise[0])
    return mixed.T, grad_tok.T, new_up[None], new_down.T[None]


def solution(mesh):
    in_specs = (
        P("expert", "dp"),
        P("expert", "dp"),
        P("expert", None),
        P("expert", None),
        P(),
        P("expert", "dp", None),
        P("expert", None, "dp"),
        P("expert", "dp", None),
    )
    out_specs = (
        P("expert", "dp"),
        P("expert", "dp"),
        P("expert", "dp", None),
        P("expert", None, "dp"),
    )
    return jax.shard_map(shards, mesh=mesh, in_specs=in_specs, out_specs=out_specs, check_vma=False)
```
